128 devices in a mesh: sfc: 128 (over y, z, x, core).
Axes of the slice: x: 4, y: 4, z: 4, core: 2. Of those that a mesh axis runs over, the one named last changes fastest.
Arguments:
- tracers: float32 [8192, 3, 480], P('sfc'), may hold values from -6 to 6
- weights: float32 [2, 8192, 3, 256], P(None, 'sfc'), may hold values from -1.5 to 1.5
- departure: int32 [8192, 48], P('sfc'), may hold values from 0 to 95, as said below
- needs: int32 [128, 8, 4], P('sfc'), may hold values from 0 to 63
- counts: int32 [128, 8], P('sfc'), may hold values from 1 to 4, as said below
Outputs:
- mixed: float32 [8192, 3, 480], P('sfc')
The draws below stay inside these ranges and needn't reach their ends.
Inputs may be any that keep to these rules, and one draw needn't show every extreme that they name: `departure`: each entry is a slot of its range's source table: below 64 a local element; otherwise 64 + j * 4 + c with c below counts[r, j] of its range r. `counts`: some range uses all 4 entries of every list in every draw.
All inputs are finite; a program needn't handle non-finite values.
Results may differ from the reference program's by a relative error of at most 0.0003.
Values sent between devices are 32-bit elements; how exact they have to be, the bound alone decides.
No kernel may reach another device: no remote copies, remote signals or barrier semaphores. Data moves between devices by JAX's collectives and lax.ppermute only.
A program may use at most 64 MiB of HBM per device.

```python
import math
import jax
import jax.numpy as jnp
from jax import lax

NODES = 16
TRACERS = 30
LEV = 3
SUBSTEPS = 2
REACH = 4
CAP = 4
ELEMS = 64
ELEMS_ALL = 8192
N_SFC = 128


def counts_table(key):
    ranks_total = ELEMS_ALL // ELEMS
    folded = jax.random.fold_in(key, 11)
    key_counts, key_band = jax.random.split(folded)
    drawn = jax.random.randint(key_counts, (ranks_total, 2 * REACH), 1, CAP + 1)
    band_start = jax.random.randint(key_band, (), 0, ranks_total)
    in_band = (jnp.arange(ranks_total) - band_start) % ranks_total < max(ranks_total // 4, 1)
    return jnp.where(in_band[:, None], CAP, drawn).astype(jnp.int32)


def draw_counts(key, part):
    return counts_table(key)


def draw_departure(key, part):
    limits_table = counts_table(key)
    folded = jax.random.fold_in(key, 23)
    key_remote, key_offset, key_column, key_local = jax.random.split(folded, 4)
    grid_shape = (ELEMS_ALL, LEV * NODES)
    owner_rank = (jnp.arange(ELEMS_ALL) // ELEMS)[:, None]
    remote = jax.random.randint(key_remote, grid_shape, 0, 10) < 3
    offset_pick = jax.random.randint(key_offset, grid_shape, 0, 2 * REACH)
    raw_bits = jax.random.randint(key_column, grid_shape, 0, 1 << 20)
    limits = limits_table[owner_rank, offset_pick]
    column = raw_bits % limits
    local_pick = jax.random.randint(key_local, grid_shape, 0, ELEMS)
    return jnp.where(remote, ELEMS + offset_pick * CAP + column, local_pick).astype(jnp.int32)


def set_ends(entries, rng, smallest, high):
    place = [jax.random.randint(jax.random.fold_in(rng, axis), (), 0, length) for axis, length in enumerate(entries.shape)]
    longest = entries.shape.index(max(entries.shape))
    next_to = place[:longest] + [(place[longest] + 1) % entries.shape[longest]] + place[longest + 1:]
    return entries.at[tuple(place)].set(smallest).at[tuple(next_to)].set(high)


def block_scale(stream_key, extent, cuts, least, top_value):
    gain = 1.0
    for position, shards_of in cuts:
        draws = jax.random.uniform(jax.random.fold_in(jax.random.fold_in(stream_key, 6), position), (shards_of,), jnp.float32, least / len(cuts), top_value / len(cuts))
        gain = gain * jnp.repeat(jnp.exp(draws), extent[position] // shards_of).reshape((-1,) + (1,) * (len(extent) - 1 - position))
    return gain


def normal_values(key, dims, spread, bound, pieces=(), held_as=jnp.bfloat16):
    values = spread * jax.random.normal(key, dims, jnp.float32)
    if pieces:
        values = values * block_scale(key, dims, pieces, -0.22, 0.18)
    return jnp.clip(values, -bound, bound).astype(held_as)


def setup_inputs(seed: int = 0) -> dict:
    seeds = jax.random.split(jax.random.key(seed), 6)
    return {
        "tracers": normal_values(seeds[0], (ELEMS_ALL, LEV, NODES * TRACERS), 1.0, 6.0, ((0, 128),), jnp.float32),
        "weights": normal_values(seeds[1], (SUBSTEPS, ELEMS_ALL, LEV, NODES * NODES), NODES ** -0.5, 1.5, ((1, 128),), jnp.float32),
        "departure": draw_departure(jax.random.fold_in(seeds[5], 71), 0),
        "needs": set_ends(jax.random.randint(seeds[3], (N_SFC, 2 * REACH, CAP), 0, ELEMS), jax.random.fold_in(seeds[3], 1), 0, ELEMS - 1).astype(jnp.int32),
        "counts": draw_counts(jax.random.fold_in(seeds[5], 71), 0),
    }


def interpolate(source_table, dep_block, weight_block):
    elements = dep_block.shape[0]
    block_rows = math.gcd(elements, 32)
    flat_rows = source_table.reshape(-1, NODES * TRACERS)
    slot_rows = dep_block.reshape(elements, LEV, NODES) * LEV + jnp.arange(LEV, dtype=jnp.int32)[None, :, None]

    def per_block(inputs):
        row_index, matrices = inputs
        gathered = flat_rows[row_index].reshape(block_rows, LEV, NODES, NODES, TRACERS)
        matrices = matrices.reshape(block_rows, LEV, NODES, NODES)
        values = jnp.einsum("elts,eltsq->eltq", matrices, gathered, precision=lax.Precision.HIGHEST)
        lowest = jnp.min(gathered, axis=3)
        highest = jnp.max(gathered, axis=3)
        return jnp.clip(values, lowest, highest).reshape(block_rows, LEV, NODES * TRACERS)

    result = lax.map(per_block, (slot_rows.reshape(elements // block_rows, block_rows, LEV, NODES),
                                 weight_block.reshape(elements // block_rows, block_rows, LEV, NODES * NODES)))
    return result.reshape(elements, LEV, NODES * TRACERS)


def reference(tracers, weights, departure, needs, counts):
    offset_order = jnp.arange(2 * REACH, dtype=jnp.int32)
    offsets = jnp.where(offset_order < REACH, offset_order - REACH, offset_order - REACH + 1)
    live_slots = jnp.arange(CAP, dtype=jnp.int32)[None, None, :] < counts[:, :, None]
    current = tracers
    for substep in range(SUBSTEPS):
        def per_range(owner_rank):
            own_rows = lax.dynamic_slice_in_dim(current, owner_rank * ELEMS, ELEMS, 0)
            owners = (owner_rank + offsets) % N_SFC
            row_index = (owners[:, None] * ELEMS + needs[owner_rank]).astype(jnp.int32)
            remote = current[row_index]
            remote = jnp.where(live_slots[owner_rank][:, :, None, None], remote, 0.0)
            source_table = jnp.concatenate([own_rows, remote.reshape(2 * REACH * CAP, LEV, NODES * TRACERS)], axis=0)
            dep_block = lax.dynamic_slice_in_dim(departure, owner_rank * ELEMS, ELEMS, 0)
            weight_block = lax.dynamic_slice_in_dim(weights[substep], owner_rank * ELEMS, ELEMS, 0)
            return interpolate(source_table, dep_block, weight_block)

        current = lax.map(per_range, jnp.arange(N_SFC, dtype=jnp.int32)).reshape(ELEMS_ALL, LEV, NODES * TRACERS)
    return current
```

```python
import jax
import jax.numpy as jnp
from jax import lax
from jax.experimental import pallas as pl
from jax.experimental.pallas import tpu as pltpu
from jax.sharding import PartitionSpec as P


NODES = 16
TRACERS = 30
LEV = 3
SUBSTEPS = 2
REACH = 4
CAP = 4
ELEMS = 64
ROW = NODES * TRACERS
WIDE = 32
TALL = NODES * WIDE
REMOTE = 2 * REACH * CAP
DEPTH = 2 * ELEMS + 2 * REMOTE
PAIRS = 4
LANES = 128
N = 128


VMEM = pl.BlockSpec(memory_space=pltpu.VMEM)
HBM = pl.BlockSpec(memory_space=pltpu.HBM)
SMEM = pl.BlockSpec(memory_space=pltpu.SMEM)
f32 = jnp.float32
bf16 = jnp.bfloat16


def moved(value, target):
    return lax.ppermute(value, "sfc", [(source, target(source) % N) for source in range(N)])


def swapped(value):
    return moved(value, lambda device: device ^ 1)


def ahead(value, chips):
    return moved(value, lambda device: device + 2 * chips * (1 - 2 * (device % 2)))


def split(x):
    high = x.astype(bf16).astype(f32)
    return high, x - high


def prepare(me, counts_in, tracers_in, weights_in, departure_in, table, hot, turned, tracers,
            spaced, counts, weights, departure, done):
    copies = [pltpu.make_async_copy(source, target, done.at[i]) for i, (source, target) in enumerate(
        [(tracers_in, tracers), (counts_in, counts), (departure_in, departure), (weights_in, weights)])]
    for copy in copies:
        copy.start()
    spaced[ROW:, :] = jnp.zeros_like(spaced[ROW:, :])
    copies[0].wait()
    copies[1].wait()
    copies[2].wait()
    slot = lax.broadcasted_iota(jnp.int32, (REMOTE, LANES), 0)
    group, entry = slot // CAP, slot % CAP
    limit = base = jnp.zeros_like(slot)
    for q in range(2 * REACH):
        j = jnp.where(me[0] == 0, HELD[0][q], HELD[1][q])
        limit = jnp.where(group == q, counts[0, j], limit)
        base = jnp.where(group == q, ELEMS + j * CAP, base)
    far_slot = jnp.where(entry < limit, base + entry, -1)
    near_slot = lax.broadcasted_iota(jnp.int32, (ELEMS, LANES), 0)
    for level in range(LEV):
        high, low = split(tracers[level])
        spaced[0:ROW, :] = jnp.concatenate([high, low], axis=0).T
        for k in range(NODES):
            table[level, k * WIDE:(k + 1) * WIDE, :] = spaced[k * TRACERS:k * TRACERS + WIDE, :].astype(bf16)
        upper = departure[level * NODES:level * NODES + 8, :]
        lower = departure[level * NODES + 8:level * NODES + 16, :]
        wanted = jnp.concatenate([upper, lower], axis=1)
        for t in range(8):
            row = wanted[t:t + 1, :]
            near = (near_slot == row).astype(f32).astype(bf16)
            far = (far_slot == row).astype(f32).astype(bf16)
            lanes = slice((t % 2) * LANES, (t % 2 + 1) * LANES)
            hot[level, t // 2, :, lanes] = jnp.concatenate([near, near, far, far], axis=0)
    copies[3].wait()
    for level in range(LEV):
        for step in range(SUBSTEPS):
            both = jnp.concatenate([weights[step, level, :, 0:LANES], weights[step, level, :, LANES:2 * LANES]], axis=0)
            turned[step, level] = both.T


def pack(width, me, asked2, asked1, lists, own, other, near, far, inner):
    lane = lax.broadcasted_iota(jnp.int32, (CAP, LANES), 1)
    sources = [asked1.at[0], asked1.at[1], asked2.at[0], asked2.at[1], lists]
    picks = []
    for source, first, second in PACKED:
        one = [sources[source][:, j:j + 1] + ELEMS * place for j, place in (first, second)]
        picks.append((jnp.broadcast_to(jnp.where(me[0] == 0, one[0], one[1]), (CAP, LANES)) == lane).astype(f32))
    picks = jnp.concatenate(picks, axis=0).astype(bf16)
    picks = jnp.concatenate([picks, picks, picks], axis=1)

    def give(level, lanes, rows):
        near[0, level, :, lanes] = rows[0:8]
        near[1, level, :, lanes] = rows[8:16]
        for g in range(3):
            far[g, level, :, lanes] = rows[16 + 4 * g:20 + 4 * g]
        inner[level, :, lanes] = rows[28:32]

    for level in range(LEV):
        both = jnp.concatenate([own[level], other[level]], axis=0)
        high, rest = split(both)
        middle, low = split(rest)
        parts = jnp.concatenate([high.astype(bf16), middle.astype(bf16), low.astype(bf16)], axis=0)
        rows = jnp.dot(picks, parts, preferred_element_type=f32)
        if width == TALL:
            give(level, slice(0, TALL), rows)
        else:
            spread = []
            for k in range(NODES):
                spread += [rows[:, k * TRACERS:(k + 1) * TRACERS], jnp.zeros((REMOTE, WIDE - TRACERS), f32)]
            give(level, slice(0, TALL), jnp.concatenate(spread, axis=1))


def substep(step, near, far, near_other, far_other, inner, table, hot, turned, out, whole, mixed, close):
    last = step + 1 == SUBSTEPS
    for level in range(LEV):
        rows = jnp.concatenate(
            [near[0, level], far[0, level], near_other[1, level], far_other[1, level], far_other[2, level], inner[level]],
            axis=0)
        high, low = split(rows)
        whole[level, :, 0:2 * ELEMS] = table[level]
        whole[level, :, 2 * ELEMS:] = jnp.concatenate([high, low], axis=0).T.astype(bf16)

    for level in range(LEV):
        for pair in range(PAIRS):
            gathered = jnp.dot(whole[level], hot[level, pair], preferred_element_type=f32)
            for half in range(2):
                lanes = slice(half * LANES, (half + 1) * LANES)
                t = pair * 2 + half
                factors = turned[step, level, t * NODES:(t + 1) * NODES, :]
                total = lowest = highest = None
                for k in range(NODES):
                    piece = gathered[k * WIDE:(k + 1) * WIDE, lanes]
                    term = piece * factors[k:k + 1, :]
                    total = term if k == 0 else total + term
                    lowest = piece if k == 0 else jnp.minimum(lowest, piece)
                    highest = piece if k == 0 else jnp.maximum(highest, piece)
                result = jnp.minimum(jnp.maximum(total, lowest), highest)
                if last:
                    close[level, t * TRACERS:(t + 1) * TRACERS, :] = result[:TRACERS]
                else:
                    mixed[level, t * WIDE:(t + 1) * WIDE, :] = result
        if last:
            rows = close[level].T
            half = 8 * TRACERS
            out[level, :, 0:half] = rows[:ELEMS, 0:half]
            out[level, :, half:2 * half] = rows[ELEMS:, 0:half]
        else:
            rows = mixed[level].T
            out[level, :, 0:8 * WIDE] = rows[:ELEMS]
            out[level, :, 8 * WIDE:] = rows[ELEMS:]


def retable(tracers, table):
    for level in range(LEV):
        high, low = split(tracers[level])
        table[level] = jnp.concatenate([high, low], axis=0).T.astype(bf16)


def shaped(*dims, dtype=f32):
    return jax.ShapeDtypeStruct(dims, dtype)


TABLE = shaped(LEV, TALL, 2 * ELEMS, dtype=bf16)
HELD = ((5, 6, 7, 2, 3, 0, 1, 4), (1, 2, 0, 4, 5, 6, 7, 3))
PACKED = (
    (0, (5, 0), (1, 1)), (0, (6, 1), (2, 0)), (1, (4, 0), (2, 1)), (1, (5, 1), (3, 0)),
    (2, (7, 0), (0, 0)), (3, (6, 0), (0, 1)), (3, (7, 1), (1, 0)), (4, (4, 1), (3, 1)),
)
SCRATCH = [
    pltpu.VMEM((LEV, TALL, DEPTH), bf16),
    pltpu.VMEM((LEV, 8 * WIDE, LANES), f32),
    pltpu.VMEM((LEV, 8 * WIDE, LANES), f32),
]


def kept(value):
    return pltpu.with_memory_space_constraint(value, pltpu.VMEM)


def join(mine, theirs, both):
    both[0] = mine[...]
    both[1] = theirs[...]


def fetch(source, target, done):
    copy = pltpu.make_async_copy(source, target, done)
    copy.start()
    copy.wait()


def call(body, inputs, outs, scratch=(), smem=(), outside=(), keep=True):
    inputs = [pltpu.with_memory_space_constraint(x, pltpu.HBM) if i in outside else x for i, x in enumerate(inputs)]
    return pl.pallas_call(
        body,
        in_specs=[SMEM if i in smem else HBM if i in outside else VMEM for i in range(len(inputs))],
        out_specs=jax.tree.map(lambda _: VMEM, outs),
        out_shape=jax.tree.map(lambda o: pltpu.VMEM(o.shape, o.dtype), outs) if keep else outs,
        scratch_shapes=list(scratch),
        compiler_params=pltpu.CompilerParams(vmem_limit_bytes=12 << 20),
    )(*inputs)


def on_device(tracers, weights, departure, needs, counts):
    me = lax.axis_index("sfc")[None] % 2
    levels = jnp.transpose(tracers, (1, 0, 2))
    lists = jnp.transpose(needs[0], (1, 0))
    partner_lists = kept(swapped(lists))
    lists = kept(call(fetch, [lists], shaped(CAP, 2 * REACH, dtype=jnp.int32), [pltpu.SemaphoreType.DMA(())],
                      outside=(0,)))
    both = kept(call(join, [lists, partner_lists], shaped(2, CAP, 2 * REACH, dtype=jnp.int32)))
    asked2 = kept(ahead(both, 2))
    asked1 = kept(ahead(both, 1))
    other = kept(swapped(levels))
    table, hot, turned, levels = map(kept, call(
        prepare,
        [me, counts, levels, jnp.transpose(weights, (0, 2, 1, 3)), jnp.transpose(departure, (1, 0))],
        (TABLE, shaped(LEV, PAIRS, DEPTH, 2 * LANES, dtype=bf16), shaped(SUBSTEPS, LEV, LANES, LANES),
         shaped(LEV, ELEMS, ROW)),
        [pltpu.VMEM((TALL, LANES), f32), pltpu.SMEM((1, 2 * REACH), jnp.int32),
         pltpu.VMEM((SUBSTEPS, LEV, ELEMS, NODES * NODES), f32), pltpu.VMEM((LEV * NODES, ELEMS), jnp.int32),
         pltpu.SemaphoreType.DMA((4,))], smem=(0,), outside=(1, 2, 3, 4)))
    asked = [asked2, asked1, lists]
    for step in range(SUBSTEPS):
        width = TALL if step else ROW
        near, far, inner = call(
            lambda *refs: pack(width, *refs), [me] + asked + [levels, other],
            (shaped(2, LEV, 2 * CAP, TALL), shaped(3, LEV, CAP, TALL), shaped(LEV, CAP, TALL)), smem=(0,))
        far = kept(ahead(far, -2))
        near = kept(ahead(near, -1))
        inner = kept(inner)
        if step:
            table = kept(call(retable, [levels], TABLE))
        far_other = kept(swapped(far))
        near_other = kept(swapped(near))
        last = step + 1 == SUBSTEPS
        levels = call(
            lambda *refs: substep(step, *refs),
            [near, far, near_other, far_other, inner, table, hot, turned],
            shaped(LEV, ELEMS, ROW if last else TALL), SCRATCH, keep=not last)
        if not last:
            levels = kept(levels)
            other = kept(swapped(levels))
    return jnp.transpose(levels, (1, 0, 2))


def solution(mesh):
    return jax.shard_map(
        on_device,
        mesh=mesh,
        in_specs=(
            P("sfc", None, None),
            P(None, "sfc", None, None),
            P("sfc", None),
            P("sfc", None, None),
            P("sfc", None),
        ),
        out_specs=P("sfc", None, None),
        check_vma=False,
    )
```

```python
import jax
import jax.numpy as jnp
from jax import lax
from jax.experimental import pallas as pl
from jax.experimental.pallas import tpu as pltpu
from jax.sharding import PartitionSpec as P


NODES = 16
TRACERS = 30
LEV = 3
SUBSTEPS = 2
REACH = 4
CAP = 4
ELEMS = 64
ROW = NODES * TRACERS
WIDE = 32
TALL = NODES * WIDE
REMOTE = 2 * REACH * CAP
DEPTH = 2 * ELEMS + 2 * REMOTE
PAIRS = 4
LANES = 128
N = 128


VMEM = pl.BlockSpec(memory_space=pltpu.VMEM)
HBM = pl.BlockSpec(memory_space=pltpu.HBM)
SMEM = pl.BlockSpec(memory_space=pltpu.SMEM)
f32 = jnp.float32
bf16 = jnp.bfloat16


def moved(value, target):
    return lax.ppermute(value, "sfc", [(source, target(source) % N) for source in range(N)])


def swapped(value):
    return moved(value, lambda device: device ^ 1)


def ahead(value, chips):
    return moved(value, lambda device: device + 2 * chips * (1 - 2 * (device % 2)))


def split(x):
    high = x.astype(bf16).astype(f32)
    return high, x - high


def prepare(me, tracers, counts_in, weights_in, departure_in, table, hot, turned,
            spaced, counts, weights, departure, done):
    copies = [pltpu.make_async_copy(source, target, done.at[i]) for i, (source, target) in enumerate(
        [(counts_in, counts), (departure_in, departure), (weights_in, weights)])]
    for copy in copies:
        copy.start()
    spaced[ROW:, :] = jnp.zeros_like(spaced[ROW:, :])
    copies[0].wait()
    copies[1].wait()
    slot = lax.broadcasted_iota(jnp.int32, (REMOTE, LANES), 0)
    group, entry = slot // CAP, slot % CAP
    limit = base = jnp.zeros_like(slot)
    for q in range(2 * REACH):
        j = jnp.where(me[0] == 0, HELD[0][q], HELD[1][q])
        limit = jnp.where(group == q, counts[0, j], limit)
        base = jnp.where(group == q, ELEMS + j * CAP, base)
    far_slot = jnp.where(entry < limit, base + entry, -1)
    near_slot = lax.broadcasted_iota(jnp.int32, (ELEMS, LANES), 0)
    for level in range(LEV):
        high, low = split(tracers[level])
        spaced[0:ROW, :] = jnp.concatenate([high, low], axis=0).T
        for k in range(NODES):
            table[level, k * WIDE:(k + 1) * WIDE, :] = spaced[k * TRACERS:k * TRACERS + WIDE, :].astype(bf16)
        upper = departure[level * NODES:level * NODES + 8, :]
        lower = departure[level * NODES + 8:level * NODES + 16, :]
        wanted = jnp.concatenate([upper, lower], axis=1)
        for t in range(8):
            row = wanted[t:t + 1, :]
            near = (near_slot == row).astype(f32).astype(bf16)
            far = (far_slot == row).astype(f32).astype(bf16)
            lanes = slice((t % 2) * LANES, (t % 2 + 1) * LANES)
            hot[level, t // 2, :, lanes] = jnp.concatenate([near, near, far, far], axis=0)
    copies[2].wait()
    for level in range(LEV):
        for step in range(SUBSTEPS):
            both = jnp.concatenate([weights[step, level, :, 0:LANES], weights[step, level, :, LANES:2 * LANES]], axis=0)
            turned[step, level] = both.T


def pack(me, asked2, asked1, lists, own, other, near, far, inner):
    lane = lax.broadcasted_iota(jnp.int32, (CAP, LANES), 1)
    sources = [asked1.at[0], asked1.at[1], asked2.at[0], asked2.at[1], lists]
    picks = []
    for source, first, second in PACKED:
        one = [sources[source][:, j:j + 1] + ELEMS * place for j, place in (first, second)]
        picks.append((jnp.broadcast_to(jnp.where(me[0] == 0, one[0], one[1]), (CAP, LANES)) == lane).astype(f32))
    picks = jnp.concatenate(picks, axis=0).astype(bf16)
    picks = jnp.concatenate([picks, picks, picks], axis=1)
    for level in range(LEV):
        high, rest = split(jnp.concatenate([own[level], other[level]], axis=0))
        middle, low = split(rest)
        parts = jnp.concatenate([high.astype(bf16), middle.astype(bf16), low.astype(bf16)], axis=0)
        rows = jnp.dot(picks, parts, preferred_element_type=f32)
        near[0, level] = rows[0:8]
        near[1, level] = rows[8:16]
        for g in range(3):
            far[g, level] = rows[16 + 4 * g:20 + 4 * g]
        inner[level] = rows[28:32]


def substep(step, near, far, near_other, far_other, inner, table, hot, turned, out, whole, mixed, close, spaced, rowed, done):
    last = step + 1 == SUBSTEPS
    half = 8 * TRACERS
    spaced[:, ROW:, :] = jnp.zeros_like(spaced[:, ROW:, :])

    def assemble(level):
        rows = jnp.concatenate(
            [near[0, level], far[0, level], near_other[1, level], far_other[1, level], far_other[2, level], inner[level]],
            axis=0)
        high, low = split(rows)
        whole[level, :, 0:2 * ELEMS] = table[level]
        columns = jnp.concatenate([high, low], axis=0).T
        if step:
            whole[level, :, 2 * ELEMS:] = columns.astype(bf16)
        else:
            spaced[level, 0:ROW, :] = columns
            for k in range(NODES):
                whole[level, k * WIDE:(k + 1) * WIDE, 2 * ELEMS:] = spaced[
                    level, k * TRACERS:k * TRACERS + WIDE, :].astype(bf16)

    def give(level):
        if last:
            rows = close[level].T
            rowed[level, :, 0:half] = rows[:ELEMS, 0:half]
            rowed[level, :, half:2 * half] = rows[ELEMS:, 0:half]
            pltpu.make_async_copy(rowed.at[level], out.at[level], done.at[level]).start()
        else:
            rows = mixed[level].T
            out[level, :, 0:8 * WIDE] = rows[:ELEMS]
            out[level, :, 8 * WIDE:] = rows[ELEMS:]

    for level in range(LEV):
        assemble(level)
    for level in range(LEV):
        for pair in range(PAIRS):
            gathered = jnp.dot(whole[level], hot[level, pair], preferred_element_type=f32)
            for side in range(2):
                lanes = slice(side * LANES, (side + 1) * LANES)
                t = pair * 2 + side
                factors = turned[step, level, t * NODES:(t + 1) * NODES, :]
                total = lowest = highest = None
                for k in range(NODES):
                    piece = gathered[k * WIDE:(k + 1) * WIDE, lanes]
                    term = piece * factors[k:k + 1, :]
                    total = term if k == 0 else total + term
                    lowest = piece if k == 0 else jnp.minimum(lowest, piece)
                    highest = piece if k == 0 else jnp.maximum(highest, piece)
                result = jnp.minimum(jnp.maximum(total, lowest), highest)
                if last:
                    close[level, t * TRACERS:(t + 1) * TRACERS, :] = result[:TRACERS]
                else:
                    mixed[level, t * WIDE:(t + 1) * WIDE, :] = result
        give(level)
    if last:
        for level in range(LEV):
            pltpu.make_async_copy(rowed.at[level], out.at[level], done.at[level]).wait()


def retable(tracers, table):
    for level in range(LEV):
        high, low = split(tracers[level])
        table[level] = jnp.concatenate([high, low], axis=0).T.astype(bf16)


def shaped(*dims, dtype=f32):
    return jax.ShapeDtypeStruct(dims, dtype)


TABLE = shaped(LEV, TALL, 2 * ELEMS, dtype=bf16)
HELD = ((5, 6, 7, 2, 3, 0, 1, 4), (1, 2, 0, 4, 5, 6, 7, 3))
PACKED = (
    (0, (5, 0), (1, 1)), (0, (6, 1), (2, 0)), (1, (4, 0), (2, 1)), (1, (5, 1), (3, 0)),
    (2, (7, 0), (0, 0)), (3, (6, 0), (0, 1)), (3, (7, 1), (1, 0)), (4, (4, 1), (3, 1)),
)
SCRATCH = [
    pltpu.VMEM((LEV, TALL, DEPTH), bf16),
    pltpu.VMEM((LEV, 8 * WIDE, LANES), f32),
    pltpu.VMEM((LEV, 8 * WIDE, LANES), f32),
    pltpu.VMEM((LEV, TALL, 2 * REMOTE), f32),
    pltpu.VMEM((LEV, ELEMS, ROW), f32),
    pltpu.SemaphoreType.DMA((LEV,)),
]


def kept(value):
    return pltpu.with_memory_space_constraint(value, pltpu.VMEM)


def join(mine, theirs, both):
    both[0] = mine[...]
    both[1] = theirs[...]


def fetch(source, target, done):
    copy = pltpu.make_async_copy(source, target, done)
    copy.start()
    copy.wait()


def call(body, inputs, outs, scratch=(), smem=(), outside=(), keep=True):
    inputs = [pltpu.with_memory_space_constraint(x, pltpu.HBM) if i in outside else x for i, x in enumerate(inputs)]
    return pl.pallas_call(
        body,
        in_specs=[SMEM if i in smem else HBM if i in outside else VMEM for i in range(len(inputs))],
        out_specs=jax.tree.map(lambda _: VMEM if keep else HBM, outs),
        out_shape=jax.tree.map(lambda o: pltpu.VMEM(o.shape, o.dtype), outs) if keep else outs,
        scratch_shapes=list(scratch),
        compiler_params=pltpu.CompilerParams(vmem_limit_bytes=12 << 20),
    )(*inputs)


def on_device(tracers, weights, departure, needs, counts):
    me = lax.axis_index("sfc")[None] % 2
    levels = jnp.transpose(tracers, (1, 0, 2))
    lists = jnp.transpose(needs[0], (1, 0))
    partner_lists = kept(swapped(lists))
    other = kept(swapped(levels))
    lists = kept(call(fetch, [lists], shaped(CAP, 2 * REACH, dtype=jnp.int32), [pltpu.SemaphoreType.DMA(())],
                      outside=(0,)))
    both = kept(call(join, [lists, partner_lists], shaped(2, CAP, 2 * REACH, dtype=jnp.int32)))
    asked2 = kept(ahead(both, 2))
    asked1 = kept(ahead(both, 1))
    asked = [asked2, asked1, lists]
    levels = kept(call(fetch, [levels], shaped(LEV, ELEMS, ROW), [pltpu.SemaphoreType.DMA(())], outside=(0,)))
    for step in range(SUBSTEPS):
        last = step + 1 == SUBSTEPS
        width = TALL if step else ROW
        near, far, inner = call(
            lambda *refs: pack(*refs), [me] + asked + [levels, other],
            (shaped(2, LEV, 2 * CAP, width), shaped(3, LEV, CAP, width), shaped(LEV, CAP, width)),
            smem=(0,))
        far = kept(ahead(far, -2))
        near = kept(ahead(near, -1))
        inner = kept(inner)
        if step:
            table = kept(call(retable, [levels], TABLE))
        else:
            table, hot, turned = map(kept, call(
                prepare,
                [me, levels, counts, jnp.transpose(weights, (0, 2, 1, 3)), jnp.transpose(departure, (1, 0))],
                (TABLE, shaped(LEV, PAIRS, DEPTH, 2 * LANES, dtype=bf16), shaped(SUBSTEPS, LEV, LANES, LANES)),
                [pltpu.VMEM((TALL, LANES), f32), pltpu.SMEM((1, 2 * REACH), jnp.int32),
                 pltpu.VMEM((SUBSTEPS, LEV, ELEMS, NODES * NODES), f32), pltpu.VMEM((LEV * NODES, ELEMS), jnp.int32),
                 pltpu.SemaphoreType.DMA((3,))], smem=(0,), outside=(2, 3, 4)))
        far_other = kept(swapped(far))
        near_other = kept(swapped(near))
        levels = call(
            lambda *refs: substep(step, *refs),
            [near, far, near_other, far_other, inner, table, hot, turned],
            shaped(LEV, ELEMS, ROW if last else TALL), SCRATCH, keep=not last)
        if not last:
            levels = kept(levels)
            other = kept(swapped(levels))
    return jnp.transpose(levels, (1, 0, 2))


def solution(mesh):
    return jax.shard_map(
        on_device,
        mesh=mesh,
        in_specs=(
            P("sfc", None, None),
            P(None, "sfc", None, None),
            P("sfc", None),
            P("sfc", None, None),
            P("sfc", None),
        ),
        out_specs=P("sfc", None, None),
        check_vma=False,
    )
```

```python
import jax
import jax.numpy as jnp
from jax import lax
from jax.experimental import pallas as pl
from jax.experimental.pallas import tpu as pltpu
from jax.sharding import PartitionSpec as P


NODES = 16
TRACERS = 30
LEV = 3
SUBSTEPS = 2
REACH = 4
CAP = 4
ELEMS = 64
ROW = NODES * TRACERS
WIDE = 32
TALL = NODES * WIDE
REMOTE = 2 * REACH * CAP
DEPTH = 2 * ELEMS + 2 * REMOTE
PAIRS = 4
LANES = 128
N = 128


VMEM = pl.BlockSpec(memory_space=pltpu.VMEM)
HBM = pl.BlockSpec(memory_space=pltpu.HBM)
SMEM = pl.BlockSpec(memory_space=pltpu.SMEM)
f32 = jnp.float32
bf16 = jnp.bfloat16


def moved(value, target):
    return lax.ppermute(value, "sfc", [(source, target(source) % N) for source in range(N)])


def swapped(value):
    return moved(value, lambda device: device ^ 1)


def ahead(value, chips):
    return moved(value, lambda device: device + 2 * chips * (1 - 2 * (device % 2)))


def split(x):
    high = x.astype(bf16).astype(f32)
    return high, x - high


def prepare(me, tracers, counts_in, weights_in, departure_in, table, hot, turned,
            spaced, counts, weights, departure, done):
    copies = [pltpu.make_async_copy(source, target, done.at[i]) for i, (source, target) in enumerate(
        [(counts_in, counts), (departure_in, departure), (weights_in, weights)])]
    for copy in copies:
        copy.start()
    spaced[ROW:, :] = jnp.zeros_like(spaced[ROW:, :])
    copies[0].wait()
    copies[1].wait()
    slot = lax.broadcasted_iota(jnp.int32, (REMOTE, LANES), 0)
    group, entry = slot // CAP, slot % CAP
    limit = base = jnp.zeros_like(slot)
    for q in range(2 * REACH):
        j = jnp.where(me[0] == 0, HELD[0][q], HELD[1][q])
        limit = jnp.where(group == q, counts[0, j], limit)
        base = jnp.where(group == q, ELEMS + j * CAP, base)
    far_slot = jnp.where(entry < limit, base + entry, -1)
    near_slot = lax.broadcasted_iota(jnp.int32, (ELEMS, LANES), 0)
    for level in range(LEV):
        high, low = split(tracers[level])
        spaced[0:ROW, :] = jnp.concatenate([high, low], axis=0).T
        for k in range(NODES):
            table[level, k * WIDE:(k + 1) * WIDE, :] = spaced[k * TRACERS:k * TRACERS + WIDE, :].astype(bf16)
        upper = departure[level * NODES:level * NODES + 8, :]
        lower = departure[level * NODES + 8:level * NODES + 16, :]
        wanted = jnp.concatenate([upper, lower], axis=1)
        for t in range(8):
            row = wanted[t:t + 1, :]
            near = (near_slot == row).astype(f32).astype(bf16)
            far = (far_slot == row).astype(f32).astype(bf16)
            lanes = slice((t % 2) * LANES, (t % 2 + 1) * LANES)
            hot[level, t // 2, :, lanes] = jnp.concatenate([near, near, far, far], axis=0)
    copies[2].wait()
    for level in range(LEV):
        for step in range(SUBSTEPS):
            both = jnp.concatenate([weights[step, level, :, 0:LANES], weights[step, level, :, LANES:2 * LANES]], axis=0)
            turned[step, level] = both.T


def chosen(core, groups, sources):
    lane = lax.broadcasted_iota(jnp.int32, (CAP, ELEMS), 1)
    rows = []
    for source, low, high in groups:
        lists = sources[source]
        wanted = jnp.where(core == 0, lists[:, low:low + 1], lists[:, high:high + 1])
        rows.append((jnp.broadcast_to(wanted, (CAP, ELEMS)) == lane).astype(f32))
    return jnp.concatenate(rows, axis=0).astype(bf16)


def picked(picks, rows):
    high, rest = split(rows)
    middle, low = split(rest)
    parts = jnp.concatenate([high.astype(bf16), middle.astype(bf16), low.astype(bf16)], axis=0)
    return jnp.dot(jnp.concatenate([picks, picks, picks], axis=1), parts, preferred_element_type=f32)


def lay(level, mine, lent, near, far, inner):
    for i in range(2):
        near[i, level, 0:CAP] = mine[i * CAP:(i + 1) * CAP]
        near[i, level, CAP:2 * CAP] = lent[i * CAP:(i + 1) * CAP]
        far[i, level] = mine[(2 + i) * CAP:(3 + i) * CAP]
    far[2, level] = lent[2 * CAP:3 * CAP]
    inner[level] = lent[3 * CAP:4 * CAP]


def pack(me, asked2, asked1, lists, own, other, near, far, inner):
    sources = [asked1.at[0], asked1.at[1], asked2.at[0], asked2.at[1], lists]
    none = jnp.zeros((4 * CAP, ELEMS), bf16)
    picks = jnp.concatenate([jnp.concatenate([chosen(me[0], OWN, sources), none], axis=1),
                             jnp.concatenate([none, chosen(me[0], LENT, sources)], axis=1)], axis=0)
    for level in range(LEV):
        rows = picked(picks, jnp.concatenate([own[level], other[level]], axis=0))
        lay(level, rows[0:4 * CAP], rows[4 * CAP:8 * CAP], near, far, inner)


def choose(me, asked2, asked1, lists2, lists1, lists, picks):
    both = [chosen(me[0], OWN, [asked1.at[0], asked1.at[1], asked2.at[0], asked2.at[1]]),
            chosen(1 - me[0], LENT, [lists1.at[0], lists1.at[1], lists2.at[0], lists2.at[1], lists])]
    picks[...] = jnp.concatenate(both, axis=0)


def pick(picks, rows, mine, lent):
    for level in range(LEV):
        both = picked(picks[...], rows[level])
        mine[level] = both[0:4 * CAP]
        lent[level] = both[4 * CAP:8 * CAP]


def merge(mine, lent, near, far, inner):
    for level in range(LEV):
        lay(level, mine[level], lent[level], near, far, inner)


def substep(step, near, far, near_other, far_other, inner, table, hot, turned, *refs):
    last = step + 1 == SUBSTEPS
    out, whole, mixed, close, spaced, rowed, done = refs
    half = 8 * TRACERS
    spaced[:, ROW:, :] = jnp.zeros_like(spaced[:, ROW:, :])

    def assemble(level):
        rows = jnp.concatenate(
            [near[0, level], far[0, level], near_other[1, level], far_other[1, level], far_other[2, level], inner[level]],
            axis=0)
        high, low = split(rows)
        whole[level, :, 0:2 * ELEMS] = table[level]
        columns = jnp.concatenate([high, low], axis=0).T
        if step:
            whole[level, :, 2 * ELEMS:] = columns.astype(bf16)
        else:
            spaced[level, 0:ROW, :] = columns
            for k in range(NODES):
                whole[level, k * WIDE:(k + 1) * WIDE, 2 * ELEMS:] = spaced[
                    level, k * TRACERS:k * TRACERS + WIDE, :].astype(bf16)

    def give(level):
        if last:
            rows = close[level].T
            rowed[level, :, 0:half] = rows[:ELEMS, 0:half]
            rowed[level, :, half:2 * half] = rows[ELEMS:, 0:half]
            pltpu.make_async_copy(rowed.at[level], out.at[level], done.at[level]).start()
        else:
            rows = mixed[level].T
            out[level, :, 0:8 * WIDE] = rows[:ELEMS]
            out[level, :, 8 * WIDE:] = rows[ELEMS:]

    for level in range(LEV):
        assemble(level)
    for level in range(LEV):
        for pair in range(PAIRS):
            gathered = jnp.dot(whole[level], hot[level, pair], preferred_element_type=f32)
            for side in range(2):
                lanes = slice(side * LANES, (side + 1) * LANES)
                t = pair * 2 + side
                factors = turned[step, level, t * NODES:(t + 1) * NODES, :]
                total = lowest = highest = None
                for k in range(NODES):
                    piece = gathered[k * WIDE:(k + 1) * WIDE, lanes]
                    term = piece * factors[k:k + 1, :]
                    total = term if k == 0 else total + term
                    lowest = piece if k == 0 else jnp.minimum(lowest, piece)
                    highest = piece if k == 0 else jnp.maximum(highest, piece)
                result = jnp.minimum(jnp.maximum(total, lowest), highest)
                if last:
                    close[level, t * TRACERS:(t + 1) * TRACERS, :] = result[:TRACERS]
                else:
                    mixed[level, t * WIDE:(t + 1) * WIDE, :] = result
        give(level)
    if last:
        for level in range(LEV):
            pltpu.make_async_copy(rowed.at[level], out.at[level], done.at[level]).wait()


def retable(tracers, table):
    for level in range(LEV):
        high, low = split(tracers[level])
        table[level] = jnp.concatenate([high, low], axis=0).T.astype(bf16)


def shaped(*dims, dtype=f32):
    return jax.ShapeDtypeStruct(dims, dtype)


TABLE = shaped(LEV, TALL, 2 * ELEMS, dtype=bf16)
HELD = ((5, 6, 7, 3, 2, 1, 0, 4), (2, 1, 0, 4, 5, 6, 7, 3))
OWN = ((0, 5, 2), (1, 4, 3), (2, 7, 0), (3, 6, 1))
LENT = ((0, 6, 1), (1, 5, 2), (3, 7, 0), (4, 4, 3))
SCRATCH = [
    pltpu.VMEM((LEV, TALL, DEPTH), bf16),
    pltpu.VMEM((LEV, 8 * WIDE, LANES), f32),
    pltpu.VMEM((LEV, 8 * WIDE, LANES), f32),
    pltpu.VMEM((LEV, TALL, 2 * REMOTE), f32),
    pltpu.VMEM((LEV, ELEMS, ROW), f32),
    pltpu.SemaphoreType.DMA((LEV,)),
]


def kept(value):
    return pltpu.with_memory_space_constraint(value, pltpu.VMEM)


def join(mine, theirs, both):
    both[0] = mine[...]
    both[1] = theirs[...]


def fetch(source, target, done):
    copy = pltpu.make_async_copy(source, target, done)
    copy.start()
    copy.wait()


def call(body, inputs, outs, scratch=(), smem=(), outside=(), keep=True):
    inputs = [pltpu.with_memory_space_constraint(x, pltpu.HBM) if i in outside else x for i, x in enumerate(inputs)]
    return pl.pallas_call(
        body,
        in_specs=[SMEM if i in smem else HBM if i in outside else VMEM for i in range(len(inputs))],
        out_specs=jax.tree.map(lambda _: VMEM if keep else HBM, outs),
        out_shape=jax.tree.map(lambda o: pltpu.VMEM(o.shape, o.dtype), outs) if keep else outs,
        scratch_shapes=list(scratch),
        compiler_params=pltpu.CompilerParams(vmem_limit_bytes=12 << 20),
    )(*inputs)


def on_device(tracers, weights, departure, needs, counts):
    me = lax.axis_index("sfc")[None] % 2
    levels = jnp.transpose(tracers, (1, 0, 2))
    lists = jnp.transpose(needs[0], (1, 0))
    partner_lists = kept(swapped(lists))
    other = kept(swapped(levels))
    lists = kept(call(fetch, [lists], shaped(CAP, 2 * REACH, dtype=jnp.int32), [pltpu.SemaphoreType.DMA(())],
                      outside=(0,)))
    both = kept(call(join, [lists, partner_lists], shaped(2, CAP, 2 * REACH, dtype=jnp.int32)))
    asked2 = kept(ahead(both, 2))
    asked1 = kept(ahead(both, 1))
    asked = [asked2, asked1, lists]
    levels = kept(call(fetch, [levels], shaped(LEV, ELEMS, ROW), [pltpu.SemaphoreType.DMA(())], outside=(0,)))
    for step in range(SUBSTEPS):
        last = step + 1 == SUBSTEPS
        width = TALL if step else ROW
        pieces = (shaped(2, LEV, 2 * CAP, width), shaped(3, LEV, CAP, width), shaped(LEV, CAP, width))
        if step:
            near, far, inner = call(merge, [mine, lent], pieces)
        else:
            near, far, inner = call(pack, [me] + asked + [levels, other], pieces, smem=(0,))
        far = kept(ahead(far, -2))
        near = kept(ahead(near, -1))
        inner = kept(inner)
        if step:
            table = kept(call(retable, [levels], TABLE))
        else:
            table, hot, turned = map(kept, call(
                prepare,
                [me, levels, counts, jnp.transpose(weights, (0, 2, 1, 3)), jnp.transpose(departure, (1, 0))],
                (TABLE, shaped(LEV, PAIRS, DEPTH, 2 * LANES, dtype=bf16), shaped(SUBSTEPS, LEV, LANES, LANES)),
                [pltpu.VMEM((TALL, LANES), f32), pltpu.SMEM((1, 2 * REACH), jnp.int32),
                 pltpu.VMEM((SUBSTEPS, LEV, ELEMS, NODES * NODES), f32), pltpu.VMEM((LEV * NODES, ELEMS), jnp.int32),
                 pltpu.SemaphoreType.DMA((3,))], smem=(0,), outside=(2, 3, 4)))
        far_other = kept(swapped(far))
        near_other = kept(swapped(near))
        if not last:
            their2 = kept(swapped(asked2))
            their1 = kept(swapped(asked1))
            picks = kept(call(choose, [me, asked2, asked1, their2, their1, partner_lists],
                              shaped(8 * CAP, ELEMS, dtype=bf16), smem=(0,)))
        levels = call(
            lambda *refs: substep(step, *refs),
            [near, far, near_other, far_other, inner, table, hot, turned],
            shaped(LEV, ELEMS, ROW if last else TALL), SCRATCH,
            keep=not last)
        if not last:
            levels = kept(levels)
            mine, lent = map(kept, call(pick, [picks, levels], (shaped(LEV, 4 * CAP, TALL),) * 2))
            lent = kept(swapped(lent))
    return jnp.transpose(levels, (1, 0, 2))


def solution(mesh):
    return jax.shard_map(
        on_device,
        mesh=mesh,
        in_specs=(
            P("sfc", None, None),
            P(None, "sfc", None, None),
            P("sfc", None),
            P("sfc", None, None),
            P("sfc", None),
        ),
        out_specs=P("sfc", None, None),
        check_vma=False,
    )
```

```python
import jax
import jax.numpy as jnp
from jax import lax
from jax.experimental import pallas as pl
from jax.experimental.pallas import tpu as pltpu
from jax.sharding import PartitionSpec as P


NODES = 16
TRACERS = 30
LEV = 3
SUBSTEPS = 2
REACH = 4
CAP = 4
ELEMS = 64
ROW = NODES * TRACERS
WIDE = 32
TALL = NODES * WIDE
REMOTE = 2 * REACH * CAP
DEPTH = 2 * ELEMS + 2 * REMOTE
PAIRS = 4
LANES = 128
N = 128
PLANE = 16


VMEM = pl.BlockSpec(memory_space=pltpu.VMEM)
HBM = pl.BlockSpec(memory_space=pltpu.HBM)
SMEM = pl.BlockSpec(memory_space=pltpu.SMEM)
f32 = jnp.float32
bf16 = jnp.bfloat16


def moved(value, target):
    return lax.ppermute(value, "sfc", [(source, target(source) % N) for source in range(N)])


def swapped(value):
    return moved(value, lambda device: device ^ 1)


def ahead(value, chips):
    return moved(value, lambda device: device + 2 * chips * (1 - 2 * (device % 2)))


def stepped(value):
    return moved(value, lambda device: device - 2 * PLANE if device % 2 and device // 2 % PLANE < 2 else device)


def asking(value, chips):
    def target(device):
        chip = device // 2
        if device % 2 == 0:
            return device + 2 * chips
        return 2 * (chip // PLANE * PLANE + (chip - chips) % PLANE) + 1

    return moved(value, target)


def split(x):
    high = x.astype(bf16).astype(f32)
    return high, x - high


def prepare(me, tracers, counts_in, weights_in, departure_in, table, hot, turned,
            spaced, counts, weights, departure, done):
    copies = [pltpu.make_async_copy(source, target, done.at[i]) for i, (source, target) in enumerate(
        [(counts_in, counts), (departure_in, departure), (weights_in, weights)])]
    for copy in copies:
        copy.start()
    spaced[ROW:, :] = jnp.zeros_like(spaced[ROW:, :])
    copies[0].wait()
    copies[1].wait()
    slot = lax.broadcasted_iota(jnp.int32, (REMOTE, LANES), 0)
    group, entry = slot // CAP, slot % CAP
    limit = base = jnp.zeros_like(slot)
    for q in range(2 * REACH):
        j = jnp.where(me[0] == 0, HELD[0][q], HELD[1][q])
        limit = jnp.where(group == q, counts[0, j], limit)
        base = jnp.where(group == q, ELEMS + j * CAP, base)
    far_slot = jnp.where(entry < limit, base + entry, -1)
    near_slot = lax.broadcasted_iota(jnp.int32, (ELEMS, LANES), 0)
    for level in range(LEV):
        high, low = split(tracers[level])
        spaced[0:ROW, :] = jnp.concatenate([high, low], axis=0).T
        for k in range(NODES):
            table[level, k * WIDE:(k + 1) * WIDE, :] = spaced[k * TRACERS:k * TRACERS + WIDE, :].astype(bf16)
        upper = departure[level * NODES:level * NODES + 8, :]
        lower = departure[level * NODES + 8:level * NODES + 16, :]
        wanted = jnp.concatenate([upper, lower], axis=1)
        for t in range(8):
            row = wanted[t:t + 1, :]
            near = (near_slot == row).astype(f32).astype(bf16)
            far = (far_slot == row).astype(f32).astype(bf16)
            lanes = slice((t % 2) * LANES, (t % 2 + 1) * LANES)
            hot[level, t // 2, :, lanes] = jnp.concatenate([near, near, far, far], axis=0)
    copies[2].wait()
    for level in range(LEV):
        for step in range(SUBSTEPS):
            both = jnp.concatenate([weights[step, level, :, 0:LANES], weights[step, level, :, LANES:2 * LANES]], axis=0)
            turned[step, level] = both.T


def chosen(core, groups, sources):
    lane = lax.broadcasted_iota(jnp.int32, (CAP, ELEMS), 1)
    rows = []
    for source, low, high in groups:
        lists = sources[source]
        wanted = jnp.where(core == 0, lists[:, low:low + 1], lists[:, high:high + 1])
        rows.append((jnp.broadcast_to(wanted, (CAP, ELEMS)) == lane).astype(f32))
    return jnp.concatenate(rows, axis=0).astype(bf16)


def picked(picks, rows):
    high, rest = split(rows)
    middle, low = split(rest)
    parts = jnp.concatenate([high.astype(bf16), middle.astype(bf16), low.astype(bf16)], axis=0)
    return jnp.dot(jnp.concatenate([picks, picks, picks], axis=1), parts, preferred_element_type=f32)


def lay(level, mine, lent, near, far, inner):
    for i in range(2):
        near[i, level, 0:CAP] = mine[i * CAP:(i + 1) * CAP]
        near[i, level, CAP:2 * CAP] = lent[i * CAP:(i + 1) * CAP]
        far[i, level] = mine[(2 + i) * CAP:(3 + i) * CAP]
    far[2, level] = lent[2 * CAP:3 * CAP]
    inner[level] = lent[3 * CAP:4 * CAP]


def pack(me, asked2, asked1, lists, own, other, near, far, inner):
    sources = [asked1.at[0], asked1.at[1], asked2.at[0], asked2.at[1], lists]
    none = jnp.zeros((4 * CAP, ELEMS), bf16)
    picks = jnp.concatenate([jnp.concatenate([chosen(me[0], OWN, sources), none], axis=1),
                             jnp.concatenate([none, chosen(me[0], LENT, sources)], axis=1)], axis=0)
    for level in range(LEV):
        rows = picked(picks, jnp.concatenate([own[level], other[level]], axis=0))
        lay(level, rows[0:4 * CAP], rows[4 * CAP:8 * CAP], near, far, inner)


def choose(me, asked2, asked1, lists2, lists1, lists, picks):
    both = [chosen(me[0], OWN, [asked1.at[0], asked1.at[1], asked2.at[0], asked2.at[1]]),
            chosen(1 - me[0], LENT, [lists1.at[0], lists1.at[1], lists2.at[0], lists2.at[1], lists])]
    picks[...] = jnp.concatenate(both, axis=0)


def pick(picks, rows, mine, lent):
    for level in range(LEV):
        both = picked(picks[...], rows[level])
        mine[level] = both[0:4 * CAP]
        lent[level] = both[4 * CAP:8 * CAP]


def merge(mine, lent, near, far, inner):
    for level in range(LEV):
        lay(level, mine[level], lent[level], near, far, inner)


def substep(step, near, far, near_other, far_other, inner, table, hot, turned, *refs):
    last = step + 1 == SUBSTEPS
    out, whole, mixed, close, spaced, rowed, done = refs
    half = 8 * TRACERS
    spaced[:, ROW:, :] = jnp.zeros_like(spaced[:, ROW:, :])

    def assemble(level):
        rows = jnp.concatenate(
            [near[0, level], far[0, level], near_other[1, level], far_other[1, level], far_other[2, level], inner[level]],
            axis=0)
        high, low = split(rows)
        whole[level, :, 0:2 * ELEMS] = table[level]
        columns = jnp.concatenate([high, low], axis=0).T
        if step:
            whole[level, :, 2 * ELEMS:] = columns.astype(bf16)
        else:
            spaced[level, 0:ROW, :] = columns
            for k in range(NODES):
                whole[level, k * WIDE:(k + 1) * WIDE, 2 * ELEMS:] = spaced[
                    level, k * TRACERS:k * TRACERS + WIDE, :].astype(bf16)

    def give(level):
        if last:
            rows = close[level].T
            rowed[level, :, 0:half] = rows[:ELEMS, 0:half]
            rowed[level, :, half:2 * half] = rows[ELEMS:, 0:half]
            pltpu.make_async_copy(rowed.at[level], out.at[level], done.at[level]).start()
        else:
            rows = mixed[level].T
            out[level, :, 0:8 * WIDE] = rows[:ELEMS]
            out[level, :, 8 * WIDE:] = rows[ELEMS:]

    for level in range(LEV):
        assemble(level)
    for level in range(LEV):
        for pair in range(PAIRS):
            gathered = jnp.dot(whole[level], hot[level, pair], preferred_element_type=f32)
            for side in range(2):
                lanes = slice(side * LANES, (side + 1) * LANES)
                t = pair * 2 + side
                factors = turned[step, level, t * NODES:(t + 1) * NODES, :]
                total = lowest = highest = None
                for k in range(NODES):
                    piece = gathered[k * WIDE:(k + 1) * WIDE, lanes]
                    term = piece * factors[k:k + 1, :]
                    total = term if k == 0 else total + term
                    lowest = piece if k == 0 else jnp.minimum(lowest, piece)
                    highest = piece if k == 0 else jnp.maximum(highest, piece)
                result = jnp.minimum(jnp.maximum(total, lowest), highest)
                if last:
                    close[level, t * TRACERS:(t + 1) * TRACERS, :] = result[:TRACERS]
                else:
                    mixed[level, t * WIDE:(t + 1) * WIDE, :] = result
        give(level)
    if last:
        for level in range(LEV):
            pltpu.make_async_copy(rowed.at[level], out.at[level], done.at[level]).wait()


def retable(tracers, table):
    for level in range(LEV):
        high, low = split(tracers[level])
        table[level] = jnp.concatenate([high, low], axis=0).T.astype(bf16)


def shaped(*dims, dtype=f32):
    return jax.ShapeDtypeStruct(dims, dtype)


TABLE = shaped(LEV, TALL, 2 * ELEMS, dtype=bf16)
HELD = ((5, 6, 7, 3, 2, 1, 0, 4), (2, 1, 0, 4, 5, 6, 7, 3))
OWN = ((0, 5, 2), (1, 4, 3), (2, 7, 0), (3, 6, 1))
LENT = ((0, 6, 1), (1, 5, 2), (3, 7, 0), (4, 4, 3))
SCRATCH = [
    pltpu.VMEM((LEV, TALL, DEPTH), bf16),
    pltpu.VMEM((LEV, 8 * WIDE, LANES), f32),
    pltpu.VMEM((LEV, 8 * WIDE, LANES), f32),
    pltpu.VMEM((LEV, TALL, 2 * REMOTE), f32),
    pltpu.VMEM((LEV, ELEMS, ROW), f32),
    pltpu.SemaphoreType.DMA((LEV,)),
]


def kept(value):
    return pltpu.with_memory_space_constraint(value, pltpu.VMEM)


def join(mine, theirs, both):
    both[0] = mine[...]
    both[1] = theirs[...]


def first_leg(place, both, moved_lists, out):
    out[...] = jnp.where(place[0] == 1, moved_lists[...], both[...])


def fetch(source, target, done):
    copy = pltpu.make_async_copy(source, target, done)
    copy.start()
    copy.wait()


def call(body, inputs, outs, scratch=(), smem=(), outside=(), keep=True):
    inputs = [pltpu.with_memory_space_constraint(x, pltpu.HBM) if i in outside else x for i, x in enumerate(inputs)]
    return pl.pallas_call(
        body,
        in_specs=[SMEM if i in smem else HBM if i in outside else VMEM for i in range(len(inputs))],
        out_specs=jax.tree.map(lambda _: VMEM if keep else HBM, outs),
        out_shape=jax.tree.map(lambda o: pltpu.VMEM(o.shape, o.dtype), outs) if keep else outs,
        scratch_shapes=list(scratch),
        compiler_params=pltpu.CompilerParams(vmem_limit_bytes=12 << 20),
    )(*inputs)


def on_device(tracers, weights, departure, needs, counts):
    me = lax.axis_index("sfc")[None] % 2
    place = lax.axis_index("sfc")[None] % (2 * PLANE)
    levels = jnp.transpose(tracers, (1, 0, 2))
    lists = jnp.transpose(needs[0], (1, 0))
    partner_lists = kept(swapped(lists))
    other = kept(swapped(levels))
    lists = kept(call(fetch, [lists], shaped(CAP, 2 * REACH, dtype=jnp.int32), [pltpu.SemaphoreType.DMA(())],
                      outside=(0,)))
    both = kept(call(join, [lists, partner_lists], shaped(2, CAP, 2 * REACH, dtype=jnp.int32)))
    moved_lists = kept(stepped(both))
    one = kept(call(first_leg, [place, both, moved_lists], shaped(2, CAP, 2 * REACH, dtype=jnp.int32), smem=(0,)))
    asked2 = kept(asking(moved_lists, 2))
    asked1 = kept(asking(one, 1))
    asked = [asked2, asked1, lists]
    levels = kept(call(fetch, [levels], shaped(LEV, ELEMS, ROW), [pltpu.SemaphoreType.DMA(())], outside=(0,)))
    for step in range(SUBSTEPS):
        last = step + 1 == SUBSTEPS
        width = TALL if step else ROW
        pieces = (shaped(2, LEV, 2 * CAP, width), shaped(3, LEV, CAP, width), shaped(LEV, CAP, width))
        if step:
            near, far, inner = call(merge, [mine, lent], pieces)
        else:
            near, far, inner = call(pack, [me] + asked + [levels, other], pieces, smem=(0,))
        far = kept(ahead(far, -2))
        near = kept(ahead(near, -1))
        inner = kept(inner)
        if step:
            table = kept(call(retable, [levels], TABLE))
        else:
            table, hot, turned = map(kept, call(
                prepare,
                [me, levels, counts, jnp.transpose(weights, (0, 2, 1, 3)), jnp.transpose(departure, (1, 0))],
                (TABLE, shaped(LEV, PAIRS, DEPTH, 2 * LANES, dtype=bf16), shaped(SUBSTEPS, LEV, LANES, LANES)),
                [pltpu.VMEM((TALL, LANES), f32), pltpu.SMEM((1, 2 * REACH), jnp.int32),
                 pltpu.VMEM((SUBSTEPS, LEV, ELEMS, NODES * NODES), f32), pltpu.VMEM((LEV * NODES, ELEMS), jnp.int32),
                 pltpu.SemaphoreType.DMA((3,))], smem=(0,), outside=(2, 3, 4)))
        far_other = kept(swapped(far))
        near_other = kept(swapped(near))
        if not last:
            their2 = kept(swapped(asked2))
            their1 = kept(swapped(asked1))
            picks = kept(call(choose, [me, asked2, asked1, their2, their1, partner_lists],
                              shaped(8 * CAP, ELEMS, dtype=bf16), smem=(0,)))
        levels = call(
            lambda *refs: substep(step, *refs),
            [near, far, near_other, far_other, inner, table, hot, turned],
            shaped(LEV, ELEMS, ROW if last else TALL), SCRATCH,
            keep=not last)
        if not last:
            levels = kept(levels)
            mine, lent = map(kept, call(pick, [picks, levels], (shaped(LEV, 4 * CAP, TALL),) * 2))
            lent = kept(swapped(lent))
    return jnp.transpose(levels, (1, 0, 2))


def solution(mesh):
    return jax.shard_map(
        on_device,
        mesh=mesh,
        in_specs=(
            P("sfc", None, None),
            P(None, "sfc", None, None),
            P("sfc", None),
            P("sfc", None, None),
            P("sfc", None),
        ),
        out_specs=P("sfc", None, None),
        check_vma=False,
    )
```
